32 devices in a mesh: ctx: 8 (over z, y), tp: 4 (over x, core).
Axes of the slice: x: 2, y: 2, z: 4, core: 2. Of those that a mesh axis runs over, the one named last changes fastest.
Arguments:
- queries: bfloat16 [8192, 4096], P('ctx', 'tp'), may hold values from -6 to 6
- out_grad: bfloat16 [8192, 4096], P('ctx', 'tp'), may hold values from -6 to 6
- image_states: bfloat16 [1024, 8192], P(('ctx', 'tp')), may hold values from -6 to 6
- key_weight: bfloat16 [8192, 512], P(None, 'tp'), may hold values from -0.0625 to 0.0625
- value_weight: bfloat16 [8192, 512], P(None, 'tp'), may hold values from -0.0625 to 0.0625
- image_spans: int32 [64, 4], P('ctx'), may hold values from 0 to 31, as said below
- visible_images: int32 [8192], P('ctx'), may hold values from 1 to 4
Outputs:
- query_grad: bfloat16 [8192, 4096], P('ctx', 'tp')
- image_grad: bfloat16 [1024, 8192], P(('ctx', 'tp'))
- key_weight_grad: float32 [8192, 512], P('ctx', 'tp')
- value_weight_grad: float32 [8192, 512], P('ctx', 'tp')
The draws below stay inside these ranges and needn't reach their ends.
Inputs may be any that keep to these rules, and one draw needn't show every extreme that they name: `image_spans`: entries of a row are distinct. With c = b // 8 and j = b % 8, entry 0 of row b is c * 4 + 3 - j % 4, and every entry lies from max(c - 3, 0) * 4 to (c + 1) * 4 - 1.
All inputs are finite; a program needn't handle non-finite values.
Results may differ from the reference program's by a relative error of at most 0.014.
Values may be sent and summed in bfloat16 or wider, within the bound.
No kernel may reach another device: no remote copies, remote signals or barrier semaphores. Data moves between devices by JAX's collectives and lax.ppermute only.
A program may use at most 128 MiB of HBM per device.

```python
import jax
import jax.numpy as jnp
from jax import lax

D = 8192
QH = 32
KVH = 4
HD = 128
TXT_DEV = 1024
BLK = 128
SPAN = 4
IMG_TOK = 32
IMG_PER_DEV = 4
REACH = 3
TOKENS = 8192
TEXT_BLOCKS = 64
N_IMG = 32
IMGS = 1024


def draw_image_spans(key, part):
    blocks_total = TOKENS // BLK
    per_device = TXT_DEV // BLK
    window = (REACH + 1) * IMG_PER_DEV
    block_ids = jnp.arange(blocks_total, dtype=jnp.int32)
    device = block_ids // per_device
    first = jnp.maximum(device - REACH, 0) * IMG_PER_DEV
    own_image = device * IMG_PER_DEV + IMG_PER_DEV - 1 - block_ids % per_device % IMG_PER_DEV
    offsets = jnp.arange(window, dtype=jnp.int32)
    candidate = first[:, None] + offsets[None, :]
    usable = (candidate < (device[:, None] + 1) * IMG_PER_DEV) & (candidate != own_image[:, None])
    scores = jax.random.randint(jax.random.fold_in(key, 7), (blocks_total, window), 0, 65536)
    scores = jnp.where(usable, scores, 131072) * window + offsets[None, :]
    order = jnp.argsort(scores, axis=1)
    picked = jnp.take_along_axis(candidate, order[:, :SPAN - 1], axis=1)
    return jnp.concatenate([own_image[:, None], picked], axis=1).astype(jnp.int32)


def touch_ends(values, key, low, high):
    extent = values.shape
    place = [jax.random.randint(jax.random.fold_in(key, axis), (), 0, extent[axis]) for axis in range(len(extent))]
    values = values.at[tuple(place)].set(low)
    longest = extent.index(max(extent))
    place[longest] = (place[longest] + 1) % extent[longest]
    return values.at[tuple(place)].set(high)


def with_spikes(array, rng, source, target, shards_of, factor):
    def block_of(axis_at):
        return (jnp.arange(array.shape[axis_at]) // (array.shape[axis_at] // shards_of)).reshape((-1,) + (1,) * (array.ndim - 1 - axis_at))

    first = jax.random.permutation(rng, shards_of)[block_of(target)]
    second = (block_of(target) + shards_of // 2) % shards_of
    return jnp.where((block_of(source) == first) | (block_of(source) == second), factor * array, array)


def steps_of(key, extent, split, least, top_value):
    factor_of, own = 1.0, jax.random.fold_in(key, 6)
    for axis_at, shards_of in split:
        steps = jnp.exp(jax.random.uniform(jax.random.fold_in(own, axis_at), (shards_of,), jnp.float32, least / len(split), top_value / len(split)))
        factor_of = factor_of * jnp.repeat(steps, extent[axis_at] // shards_of).reshape([-1 if axis == axis_at else 1 for axis in range(len(extent))])
    return factor_of


def noise(key, extent, spread, reach, split=(), kind=jnp.bfloat16):
    array = spread * jax.random.normal(key, extent, jnp.float32)
    if split:
        array = array * steps_of(key, extent, split, -0.22, 0.18)
    return jnp.clip(array, -reach, reach).astype(kind)


def bell_draw_with(stream_key, shape, spread, most, pieces, heavy, kind=jnp.bfloat16):
    values = spread * jax.random.normal(stream_key, shape, jnp.float32)
    if pieces:
        values = values * steps_of(stream_key, shape, pieces, -0.22, 0.18)
    return jnp.clip(with_spikes(values, jax.random.fold_in(stream_key, 3), *heavy), -most, most).astype(kind)


def setup_inputs(seed: int = 0) -> dict:
    splits = jax.random.split(jax.random.key(seed), 8)
    return {
        "queries": noise(splits[0], (TOKENS, QH * HD), 1.0, 6.0, ((0, 8), (1, 4))),
        "out_grad": noise(splits[1], (TOKENS, QH * HD), 1.0, 6.0, ((0, 8), (1, 4))),
        "image_states": bell_draw_with(splits[2], (IMGS, D), 1.0, 6.0, ((0, 32),), (0, 1, 32, 2.75)),
        "key_weight": noise(splits[3], (D, KVH * HD), D ** -0.5, 0.0625, ((1, 4),)),
        "value_weight": noise(splits[4], (D, KVH * HD), D ** -0.5, 0.0625, ((1, 4),)),
        "image_spans": draw_image_spans(jax.random.fold_in(splits[7], 71), 0),
        "visible_images": touch_ends(jax.random.randint(splits[6], (TOKENS,), 1, SPAN + 1), jax.random.fold_in(splits[6], 1), 1, SPAN).astype(jnp.int32),
    }


epsilon = 1e-05

def normalize(inputs):
    norm_scale = lax.rsqrt(lax.optimization_barrier(jnp.mean(inputs * inputs, axis=-1, keepdims=True)) + epsilon)
    return (inputs * norm_scale, norm_scale)

def norm_back(upstream, normed, norm_scale):
    return norm_scale * (upstream - normed * lax.optimization_barrier(jnp.mean(upstream * normed, axis=-1, keepdims=True)))

def rounded(inputs):
    return lax.optimization_barrier(inputs.astype(jnp.bfloat16)).astype(jnp.float32)

def reference(queries, out_grad, image_states, key_weight, value_weight, image_spans, visible_images):
    group_size = QH // KVH
    factor = HD ** (-0.5)
    key_raw = jnp.dot(image_states, key_weight, preferred_element_type=jnp.float32).reshape(IMGS, KVH, HD)
    key_normed, key_scale = normalize(key_raw)
    key_rows = key_normed.astype(jnp.bfloat16)
    values = jnp.dot(image_states, value_weight, preferred_element_type=jnp.float32).astype(jnp.bfloat16)
    key_table = key_rows.reshape(N_IMG, IMG_TOK, KVH, HD)
    value_table = values.reshape(N_IMG, IMG_TOK, KVH, HD)
    slot_ids = jnp.arange(SPAN * IMG_TOK, dtype=jnp.int32) // IMG_TOK

    def one_block(inputs):
        query_block, grad_block, span_row, counts = inputs
        query_float = query_block.astype(jnp.float32).reshape(BLK, KVH, group_size, HD)
        query_normed, query_scale = normalize(query_float)
        query_round = rounded(query_normed)
        key_block = key_table[span_row].reshape(SPAN * IMG_TOK, KVH, HD).astype(jnp.float32)
        value_block = value_table[span_row].reshape(SPAN * IMG_TOK, KVH, HD).astype(jnp.float32)
        scores = jnp.einsum('tkgd,skd->kgts', query_round, key_block) * factor
        allowed = slot_ids[None, :] < counts[:, None]
        unnormed = jnp.where(allowed, jnp.exp(scores), 0.0)
        attention = unnormed / lax.optimization_barrier(jnp.sum(unnormed, axis=-1, keepdims=True))
        attention_round = rounded(attention)
        outputs = jnp.einsum('kgts,skd->tkgd', attention_round, value_block)
        out_grads = grad_block.astype(jnp.float32).reshape(BLK, KVH, group_size, HD)
        row_delta = jnp.transpose(lax.optimization_barrier(jnp.sum(out_grads * outputs, axis=-1)), (1, 2, 0))
        attention_grad = jnp.einsum('tkgd,skd->kgts', out_grads, value_block)
        score_grad = attention * (attention_grad - row_delta[..., None])
        score_round = rounded(score_grad)
        query_normed_grad = jnp.einsum('kgts,skd->tkgd', score_round, key_block) * factor
        query_grad = norm_back(query_normed_grad, query_normed, query_scale).astype(jnp.bfloat16)
        key_part = jnp.einsum('kgts,tkgd->skd', score_round, query_round) * factor
        value_part = jnp.einsum('kgts,tkgd->skd', attention_round, out_grads)
        return (query_grad.reshape(BLK, QH * HD), key_part, value_part)
    query_blocks = queries.reshape(TEXT_BLOCKS, BLK, QH * HD)
    grad_blocks = out_grad.reshape(TEXT_BLOCKS, BLK, QH * HD)
    count_blocks = visible_images.reshape(TEXT_BLOCKS, BLK)
    query_parts, key_parts, value_parts = lax.map(one_block, (query_blocks, grad_blocks, image_spans, count_blocks))
    flat_ids = image_spans.reshape(-1).astype(jnp.int32)
    key_normed_grad = jnp.zeros((N_IMG, IMG_TOK, KVH, HD), jnp.float32).at[flat_ids].add(key_parts.reshape(TEXT_BLOCKS * SPAN, IMG_TOK, KVH, HD))
    value_grad = jnp.zeros((N_IMG, IMG_TOK, KVH, HD), jnp.float32).at[flat_ids].add(value_parts.reshape(TEXT_BLOCKS * SPAN, IMG_TOK, KVH, HD))
    key_raw_grad = norm_back(key_normed_grad.reshape(IMGS, KVH, HD), key_normed, key_scale)
    key_round = key_raw_grad.astype(jnp.bfloat16).reshape(IMGS, KVH * HD)
    value_round = value_grad.astype(jnp.bfloat16).reshape(IMGS, KVH * HD)
    contract = (((0,), (0,)), ((), ()))
    key_weight_grad = lax.dot_general(image_states, key_round, contract, preferred_element_type=jnp.float32)
    value_weight_grad = lax.dot_general(image_states, value_round, contract, preferred_element_type=jnp.float32)
    across = (((1,), (1,)), ((), ()))
    image_grad = (lax.dot_general(key_round, key_weight, across, preferred_element_type=jnp.float32) + lax.dot_general(value_round, value_weight, across, preferred_element_type=jnp.float32)).astype(jnp.bfloat16)
    query_grad = query_parts.reshape(TOKENS, QH * HD)
    return (query_grad, image_grad, key_weight_grad, value_weight_grad)
```

```python
import functools

import jax
import jax.numpy as jnp
from jax import lax
from jax.experimental import pallas as pl
from jax.experimental.pallas import tpu as pltpu
from jax.sharding import PartitionSpec as P

HD = 128
BLK = 128
SPAN = 4
IMG_TOK = 32
IMG_PER_DEV = 4
REACH = 3
LOG2E = 1.4426950408889634

epsilon = 1e-05

f32 = jnp.float32
bf16 = jnp.bfloat16
NT = (((1,), (1,)), ((), ()))
NN = (((1,), (0,)), ((), ()))
TN = (((0,), (0,)), ((), ()))


def dot(a, b, dims):
    return lax.dot_general(a, b, dims, preferred_element_type=f32)


def shifted(block, axis, distance):
    n = lax.axis_size(axis)
    return lax.ppermute(block, axis, [(i, (i + distance) % n) for i in range(n)])


def exchanged(block, axis, mask):
    n = lax.axis_size(axis)
    return lax.ppermute(block, axis, [(i, i ^ mask) for i in range(n)])


def bits_down(n):
    bit = n // 2
    while bit:
        yield bit
        bit //= 2


def gathered(block, axis):
    pieces = {0: block}
    for bit in bits_down(lax.axis_size(axis)):
        for mask in sorted(pieces):
            pieces[mask | bit] = exchanged(pieces[mask], axis, bit)
    return [pieces[mask] for mask in sorted(pieces)]


def cost(flops, bytes_accessed):
    return pl.CostEstimate(flops=flops, bytes_accessed=bytes_accessed, transcendentals=0)


def scale_kernel(heads, q_ref, scale_ref):
    q = q_ref[...].astype(f32)
    rows = jnp.concatenate([q[:, h * HD : (h + 1) * HD] for h in range(heads)], axis=0)
    ones = jnp.ones((8, HD), f32)
    total = lax.dot_general(
        ones, rows * rows, NT, precision=lax.Precision.HIGHEST, preferred_element_type=f32
    )
    scale_ref[0] = lax.rsqrt(total[0:1] * (1.0 / HD) + epsilon)


def query_scales(queries, blocks, heads):
    width = heads * BLK
    return pl.pallas_call(
        functools.partial(scale_kernel, heads),
        grid=(blocks,),
        in_specs=[pl.BlockSpec((BLK, heads * HD), lambda b: (b, 0))],
        out_specs=pl.BlockSpec((1, 1, width), lambda b: (b, 0, 0)),
        out_shape=jax.ShapeDtypeStruct((blocks, 1, width), f32),
        cost_estimate=cost(queries.size * 100, queries.size * 2),
        name="query_scales",
    )(queries)


def project_kernel(count, steps, *refs):
    pieces = refs[:count]
    wk_ref, wv_ref, kv_ref, normed_ref, kscale_ref, acc_ref = refs[count:]
    step = pl.program_id(0)
    x = jnp.concatenate([p[...] for p in pieces], axis=0)
    w = jnp.concatenate([wk_ref[...], wv_ref[...]], axis=1)
    part = dot(x, w, NN)

    @pl.when(step == 0)
    def _():
        acc_ref[...] = part

    @pl.when(step > 0)
    def _():
        acc_ref[...] += part

    @pl.when(step == steps - 1)
    def _():
        own = lax.axis_index("tp")
        size = pieces[0].shape[0]
        for mask in range(count):
            rows = acc_ref[mask * size : (mask + 1) * size, :]
            raw = rows[:, :HD]
            scale = lax.rsqrt(jnp.mean(raw * raw, axis=-1, keepdims=True) + epsilon)
            normed = raw * scale
            there = pl.ds(pl.multiple_of((own ^ mask) * size, size), size)
            kv_ref[there, :HD] = normed.astype(bf16)
            kv_ref[there, HD:] = rows[:, HD:].astype(bf16)
            normed_ref[there, :] = normed
            kscale_ref[there, :] = jnp.broadcast_to(scale, normed.shape)


def project(pieces, key_weight, value_weight):
    count = len(pieces)
    size, depth = pieces[0].shape
    rows = count * size
    chunk = min(2048, depth)
    steps = depth // chunk
    full = lambda shape: pl.BlockSpec(shape, lambda s: (0, 0))
    return pl.pallas_call(
        functools.partial(project_kernel, count, steps),
        grid=(steps,),
        in_specs=[pl.BlockSpec((size, chunk), lambda s: (0, s))] * count
        + [pl.BlockSpec((chunk, HD), lambda s: (s, 0))] * 2,
        out_specs=[full((rows, 2 * HD)), full((rows, HD)), full((rows, HD))],
        out_shape=[
            jax.ShapeDtypeStruct((rows, 2 * HD), bf16),
            jax.ShapeDtypeStruct((rows, HD), f32),
            jax.ShapeDtypeStruct((rows, HD), f32),
        ],
        scratch_shapes=[pltpu.VMEM((rows, 2 * HD), f32)],
        cost_estimate=cost(4 * rows * depth * HD, depth * (rows + 2 * HD) * 2),
        name="project",
    )(*pieces, key_weight, value_weight)


def cited(lookup_ref, table_ref, block, column):
    return jnp.concatenate(
        [
            table_ref[pl.ds(pl.multiple_of(lookup_ref[block, s] * IMG_TOK, IMG_TOK), IMG_TOK), column : column + HD]
            for s in range(SPAN)
        ],
        axis=0,
    )


def load_table(table_ref, parts):
    size = parts[0].shape[0]
    for at, part in enumerate(parts):
        table_ref[at * size : (at + 1) * size, :] = part[...]


def attend_kernel(blocks, heads, lookup_ref, *refs):
    n = REACH + 1
    parts = refs[:n]
    q_ref, g_ref, scale_ref, seen_ref = refs[n : n + 4]
    ds_ref, coef_ref, own_ref = refs[n + 4 : n + 7]
    back_refs = refs[n + 7 : n + 7 + REACH]
    table_ref, acc_ref, att_ref = refs[n + 7 + REACH :]
    block = pl.program_id(0)
    factor = HD ** (-0.5)

    @pl.when(block == 0)
    def _():
        load_table(table_ref, parts)
        acc_ref[...] = jnp.zeros_like(acc_ref)

    keys = cited(lookup_ref, table_ref, block, 0)
    values = cited(lookup_ref, table_ref, block, HD)
    seen = seen_ref[0]
    for h in range(heads):
        at = slice(h * HD, (h + 1) * HD)
        q = q_ref[:, at]
        g = g_ref[:, at]
        scale = scale_ref[0, :, h * BLK : (h + 1) * BLK]
        scale_in = scale * factor
        raw = dot(keys, q, NT)
        grads = dot(values, g, NT)
        powers = jnp.exp2(raw * (scale_in * LOG2E))
        shown = [(seen > s).astype(f32) for s in range(SPAN)]
        total = sum(
            shown[s] * jnp.sum(powers[s * IMG_TOK : (s + 1) * IMG_TOK], axis=0, keepdims=True)
            for s in range(SPAN)
        )
        inverse = 1.0 / total
        attention = jnp.concatenate(
            [powers[s * IMG_TOK : (s + 1) * IMG_TOK] * (shown[s] * inverse) for s in range(SPAN)],
            axis=0,
        )
        delta = jnp.sum(attention * grads, axis=0, keepdims=True)
        score_grad = attention * (grads - delta) * scale_in
        coef = jnp.sum(score_grad * raw, axis=0, keepdims=True) * (scale * scale * (1.0 / HD))
        coef_ref[0, h : h + 1, :] = coef
        att_ref[:, at] = attention.astype(bf16)
        ds_ref[0, :, at] = score_grad.astype(bf16)
    q_rows = jnp.concatenate([q_ref[:, h * HD : (h + 1) * HD] for h in range(heads)], axis=0)
    g_rows = jnp.concatenate([g_ref[:, h * HD : (h + 1) * HD] for h in range(heads)], axis=0)
    key_part = dot(ds_ref[0], q_rows, NN)
    value_part = dot(att_ref[...], g_rows, NN)
    for s in range(SPAN):
        there = pl.ds(pl.multiple_of(lookup_ref[block, s] * IMG_TOK, IMG_TOK), IMG_TOK)
        here = slice(s * IMG_TOK, (s + 1) * IMG_TOK)
        acc_ref[there, :HD] += key_part[here]
        acc_ref[there, HD:] += value_part[here]

    @pl.when(block == blocks - 1)
    def _():
        size = own_ref.shape[0]
        own_ref[...] = acc_ref[:size, :]
        for at, ref in enumerate(back_refs):
            ref[...] = acc_ref[(at + 1) * size : (at + 2) * size, :].astype(bf16)


def attend(lookup, parts, queries, out_grad, scales, seen):
    blocks = lookup.shape[0]
    heads = queries.shape[1] // HD
    rows, width = parts[0].shape
    tall = heads * BLK
    full = lambda shape: pl.BlockSpec(shape, lambda b, *_: (0,) * len(shape))
    tokens = pl.BlockSpec((BLK, heads * HD), lambda b, *_: (b, 0))
    return pl.pallas_call(
        functools.partial(attend_kernel, blocks, heads),
        grid_spec=pltpu.PrefetchScalarGridSpec(
            num_scalar_prefetch=1,
            grid=(blocks,),
            in_specs=[full((rows, width))] * (REACH + 1)
            + [
                tokens,
                tokens,
                pl.BlockSpec((1, 1, tall), lambda b, *_: (b, 0, 0)),
                pl.BlockSpec((1, 1, BLK), lambda b, *_: (b, 0, 0)),
            ],
            out_specs=[
                pl.BlockSpec((1, SPAN * IMG_TOK, tall), lambda b, *_: (b, 0, 0)),
                pl.BlockSpec((1, heads, BLK), lambda b, *_: (b, 0, 0)),
            ]
            + [full((rows, width))] * (REACH + 1),
            scratch_shapes=[
                pltpu.VMEM(((REACH + 1) * rows, width), bf16),
                pltpu.VMEM(((REACH + 1) * rows, width), f32),
                pltpu.VMEM((SPAN * IMG_TOK, tall), bf16),
            ],
        ),
        out_shape=[
            jax.ShapeDtypeStruct((blocks, SPAN * IMG_TOK, tall), bf16),
            jax.ShapeDtypeStruct((blocks, heads, BLK), f32),
            jax.ShapeDtypeStruct((rows, width), f32),
        ]
        + [jax.ShapeDtypeStruct((rows, width), bf16)] * REACH,
        cost_estimate=cost(8 * queries.size * HD, queries.size * 6),
        name="attend",
    )(lookup, *parts, queries, out_grad, scales, seen)


def query_kernel(heads, lookup_ref, *refs):
    n = REACH + 1
    parts = refs[:n]
    q_ref, ds_ref, coef_ref, out_ref, table_ref = refs[n:]
    block = pl.program_id(0)

    @pl.when(block == 0)
    def _():
        load_table(table_ref, parts)

    keys = cited(lookup_ref, table_ref, block, 0)
    coef = coef_ref[0].T
    for h in range(heads):
        at = slice(h * HD, (h + 1) * HD)
        part = dot(ds_ref[0, :, at], keys, TN)
        out_ref[:, at] = (part - coef[:, h : h + 1] * q_ref[:, at].astype(f32)).astype(bf16)


def query_gradient(lookup, parts, queries, score_grads, coefs):
    blocks = lookup.shape[0]
    heads = queries.shape[1] // HD
    rows, width = parts[0].shape
    tall = heads * BLK
    full = lambda shape: pl.BlockSpec(shape, lambda b, *_: (0,) * len(shape))
    tokens = pl.BlockSpec((BLK, heads * HD), lambda b, *_: (b, 0))
    return pl.pallas_call(
        functools.partial(query_kernel, heads),
        grid_spec=pltpu.PrefetchScalarGridSpec(
            num_scalar_prefetch=1,
            grid=(blocks,),
            in_specs=[full((rows, width))] * (REACH + 1)
            + [
                tokens,
                pl.BlockSpec((1, SPAN * IMG_TOK, tall), lambda b, *_: (b, 0, 0)),
                pl.BlockSpec((1, heads, BLK), lambda b, *_: (b, 0, 0)),
            ],
            out_specs=tokens,
            scratch_shapes=[pltpu.VMEM(((REACH + 1) * rows, width), bf16)],
        ),
        out_shape=jax.ShapeDtypeStruct(queries.shape, bf16),
        cost_estimate=cost(2 * queries.size * HD, queries.size * 6),
        name="query_gradient",
    )(lookup, *parts, queries, score_grads, coefs)


def round_kernel(*refs):
    own_ref, normed_ref, kscale_ref = refs[:3]
    backs, out_ref = refs[3:-1], refs[-1]
    total = own_ref[...]
    for ref in backs:
        total = total + ref[...].astype(f32)
    normed = normed_ref[...]
    upstream = total[:, :HD]
    mean = jnp.mean(upstream * normed, axis=-1, keepdims=True)
    out_ref[:, :HD] = (kscale_ref[...] * (upstream - normed * mean)).astype(bf16)
    out_ref[:, HD:] = total[:, HD:].astype(bf16)


def round_gradients(own, backs, normed, kscale):
    return pl.pallas_call(
        round_kernel,
        out_shape=jax.ShapeDtypeStruct(own.shape, bf16),
        cost_estimate=cost(own.size * 8, own.size * 16),
        name="round_gradients",
    )(own, normed, kscale, *backs)


def image_kernel(count, rounds_ref, wk_ref, wv_ref, keep_ref, send_ref):
    own = lax.axis_index("tp")
    size = rounds_ref.shape[0] // count
    masks = sorted(range(count), key=lambda m: int(bin(m + count)[3:][::-1], 2))
    rows = jnp.concatenate(
        [rounds_ref[pl.ds(pl.multiple_of((own ^ m) * size, size), size), :] for m in masks], axis=0
    )
    total = dot(rows[:, :HD], wk_ref[...], NT) + dot(rows[:, HD:], wv_ref[...], NT)
    half = rows.shape[0] // 2
    keep_ref[...] = total[:half].astype(bf16)
    send_ref[...] = total[half:].astype(bf16)


def image_part(rounds, key_weight, value_weight, count, part, parts):
    rows, width = rounds.shape
    depth = key_weight.shape[0]
    columns = depth // parts
    chunk = min(1024, columns)
    steps = columns // chunk
    weight = pl.BlockSpec((chunk, HD), lambda s: (part * steps + s, 0))
    out = pl.BlockSpec((rows // 2, chunk), lambda s: (0, s))
    return pl.pallas_call(
        functools.partial(image_kernel, count),
        grid=(steps,),
        in_specs=[pl.BlockSpec((rows, width), lambda s: (0, 0)), weight, weight],
        out_specs=[out, out],
        out_shape=[jax.ShapeDtypeStruct((rows // 2, columns), bf16)] * 2,
        cost_estimate=cost(4 * rows * columns * HD, columns * (rows + 2 * HD) * 2),
        name="image_part",
    )(rounds, key_weight, value_weight)


def image_gradient(rounds, key_weight, value_weight, parts):
    count = lax.axis_size("tp")
    outs = []
    for part in range(parts):
        keep, send = image_part(rounds, key_weight, value_weight, count, part, parts)
        bit = 1
        while True:
            keep = keep.astype(f32) + exchanged(send, "tp", bit).astype(f32)
            bit *= 2
            if bit == count:
                break
            half = keep.shape[0] // 2
            keep, send = keep[:half], keep[half:].astype(bf16)
        outs.append(keep.astype(bf16))
    return jnp.concatenate(outs, axis=1)


def weight_kernel(count, size, *refs):
    states = refs[:count]
    rounds = refs[count:-2]
    key_ref, value_ref = refs[-2:]
    own = lax.axis_index("tp")
    total = None
    for mask in range(count):
        there = pl.ds(pl.multiple_of((own ^ mask) * size, size), size)
        rows = jnp.concatenate([r[there, :] for r in rounds], axis=0)
        part = dot(states[mask][...], rows, TN)
        total = part if total is None else total + part
    key_ref[...] = total[:, :HD]
    value_ref[...] = total[:, HD:]


def weight_gradients(states, rounds):
    count = len(states)
    tokens, columns = states[0].shape
    size = tokens // len(rounds)
    rows, width = rounds[0].shape
    chunk = min(256, columns)
    steps = columns // chunk
    out = pl.BlockSpec((chunk, HD), lambda s: (s, 0))
    return pl.pallas_call(
        functools.partial(weight_kernel, count, size),
        grid=(steps,),
        in_specs=[pl.BlockSpec((tokens, chunk), lambda s: (0, s))] * count
        + [pl.BlockSpec((rows, width), lambda s: (0, 0))] * len(rounds),
        out_specs=[out, out],
        out_shape=[jax.ShapeDtypeStruct((columns, HD), f32)] * 2,
        cost_estimate=cost(2 * count * tokens * columns * width, count * tokens * columns * 2),
        name="weight_gradients",
    )(*states, *rounds)


def on_device(
    queries, out_grad, image_states, key_weight, value_weight, image_spans, visible_images
):
    self_index = lax.axis_index("ctx")
    ctx = lax.axis_size("ctx")
    heads = queries.shape[1] // HD
    blocks = image_spans.shape[0]
    owners = image_spans // IMG_PER_DEV
    lookup = (self_index - owners) * IMG_PER_DEV + image_spans % IMG_PER_DEV
    seen = visible_images.reshape(blocks, 1, BLK)

    pieces = gathered(image_states, "tp")
    scales = query_scales(queries, blocks, heads)

    columns = image_states.shape[1] // ctx
    rows_here = image_states.shape[0]
    if ctx <= 16:
        shares = []
        for mask in range(ctx):
            start = (self_index ^ mask) * columns
            share = lax.dynamic_slice_in_dim(image_states, start, columns, axis=1)
            shares.append(exchanged(share, "ctx", mask) if mask else share)
        share = jnp.concatenate(shares, axis=0)
    else:
        share = lax.all_to_all(image_states, "ctx", split_axis=1, concat_axis=0, tiled=True)
    states = gathered(share, "tp")

    key_values, normed, kscale = project(pieces, key_weight, value_weight)
    parts = [key_values] + [shifted(key_values, "ctx", d) for d in range(1, REACH + 1)]
    score_grads, coefs, own, *windows = attend(lookup, parts, queries, out_grad, scales, seen)
    backs = [shifted(w, "ctx", -d) for d, w in enumerate(windows, 1)]
    query_grad = query_gradient(lookup, parts, queries, score_grads, coefs)
    rounds = round_gradients(own, backs, normed, kscale)
    image_grad = image_gradient(rounds, key_weight, value_weight, 4)
    if ctx <= 16:
        all_rounds = [rounds] + [exchanged(rounds, "ctx", m) for m in range(1, ctx)]
    else:
        all_rounds = list(lax.all_gather(rounds, "ctx"))
    key_weight_grad, value_weight_grad = weight_gradients(states, all_rounds)
    return (query_grad, image_grad, key_weight_grad, value_weight_grad)


def solution(mesh):
    return jax.shard_map(
        on_device,
        mesh=mesh,
        in_specs=(
            P("ctx", "tp"),
            P("ctx", "tp"),
            P(("ctx", "tp"), None),
            P(None, "tp"),
            P(None, "tp"),
            P("ctx", None),
            P("ctx"),
        ),
        out_specs=(P("ctx", "tp"), P(("ctx", "tp"), None), P("ctx", "tp"), P("ctx", "tp")),
        check_vma=False,
    )
```

```python
import functools

import jax
import jax.numpy as jnp
from jax import lax
from jax.experimental import pallas as pl
from jax.experimental.pallas import tpu as pltpu
from jax.sharding import PartitionSpec as P

HD = 128
BLK = 128
SPAN = 4
IMG_TOK = 32
IMG_PER_DEV = 4
REACH = 3
LOG2E = 1.4426950408889634
VMEM_LIMIT = 16 * 1024 * 1024

epsilon = 1e-05

f32 = jnp.float32
bf16 = jnp.bfloat16
NT = (((1,), (1,)), ((), ()))
NN = (((1,), (0,)), ((), ()))
TN = (((0,), (0,)), ((), ()))


def dot(a, b, dims):
    return lax.dot_general(a, b, dims, preferred_element_type=f32)


def shifted(block, axis, distance):
    n = lax.axis_size(axis)
    return lax.ppermute(block, axis, [(i, (i + distance) % n) for i in range(n)])


def exchanged(block, axis, mask):
    n = lax.axis_size(axis)
    return lax.ppermute(block, axis, [(i, i ^ mask) for i in range(n)])


def bits_down(n):
    bit = n // 2
    while bit:
        yield bit
        bit //= 2


def gathered(block, axis):
    pieces = {0: block}
    for bit in bits_down(lax.axis_size(axis)):
        for mask in sorted(pieces):
            pieces[mask | bit] = exchanged(pieces[mask], axis, bit)
    return [pieces[mask] for mask in sorted(pieces)]


def cost(flops, bytes_accessed):
    return pl.CostEstimate(flops=flops, bytes_accessed=bytes_accessed, transcendentals=0)


VMEM = pl.BlockSpec(memory_space=pltpu.VMEM)
SMEM = pl.BlockSpec(memory_space=pltpu.SMEM)


def call(kernel, out_shape, args, name, flops, specs=None, scratch_shapes=()):
    out_specs = [VMEM] * len(out_shape) if isinstance(out_shape, list) else VMEM
    return pl.pallas_call(
        kernel,
        in_specs=specs or [VMEM] * len(args),
        out_specs=out_specs,
        out_shape=out_shape,
        scratch_shapes=scratch_shapes,
        compiler_params=pltpu.CompilerParams(vmem_limit_bytes=VMEM_LIMIT),
        cost_estimate=cost(flops, 0),
        name=name,
    )(*args)


def rows_at(start, size):
    return pl.ds(pl.multiple_of(start, size), size)


def scale_kernel(blocks, heads, q_ref, scale_ref):
    def step(block, _):
        for h in range(heads):
            q = q_ref[rows_at(block * BLK, BLK), h * HD : (h + 1) * HD].astype(f32).T
            total = jnp.sum(q * q, axis=0, keepdims=True)
            scale_ref[block, h : h + 1, :] = lax.rsqrt(total * (1.0 / HD) + epsilon)
        return 0

    lax.fori_loop(0, blocks, step, 0)


def query_scales(queries, blocks, heads):
    return call(
        functools.partial(scale_kernel, blocks, heads),
        jax.ShapeDtypeStruct((blocks, heads, BLK), f32),
        [queries],
        "query_scales",
        queries.size * 100,
    )


def project_kernel(count, *refs):
    pieces = refs[:count]
    wk_ref, wv_ref, kv_ref, normed_ref, kscale_ref, acc_ref = refs[count:]
    size, depth = pieces[0].shape
    chunk = min(2048, depth)

    def part(start):
        at = rows_at(start, chunk)
        x = jnp.concatenate([p[:, at] for p in pieces], axis=0)
        w = jnp.concatenate([wk_ref[at, :], wv_ref[at, :]], axis=1)
        return dot(x, w, NN)

    acc_ref[...] = part(0)

    def step(i, _):
        acc_ref[...] += part(i * chunk)
        return 0

    lax.fori_loop(1, depth // chunk, step, 0)
    own = lax.axis_index("tp")
    for mask in range(count):
        rows = acc_ref[mask * size : (mask + 1) * size, :]
        raw = rows[:, :HD]
        scale = lax.rsqrt(jnp.mean(raw * raw, axis=-1, keepdims=True) + epsilon)
        normed = raw * scale
        there = rows_at((own ^ mask) * size, size)
        kv_ref[there, :HD] = normed.astype(bf16)
        kv_ref[there, HD:] = rows[:, HD:].astype(bf16)
        normed_ref[there, :] = normed
        kscale_ref[there, :] = jnp.broadcast_to(scale, normed.shape)


def project(pieces, key_weight, value_weight):
    count = len(pieces)
    size, depth = pieces[0].shape
    rows = count * size
    return call(
        functools.partial(project_kernel, count),
        [
            jax.ShapeDtypeStruct((rows, 2 * HD), bf16),
            jax.ShapeDtypeStruct((rows, HD), f32),
            jax.ShapeDtypeStruct((rows, HD), f32),
        ],
        [*pieces, key_weight, value_weight],
        "project",
        4 * rows * depth * HD,
        scratch_shapes=[pltpu.VMEM((rows, 2 * HD), f32)],
    )


def cited(lookup_ref, table_ref, block, column):
    return jnp.concatenate(
        [
            table_ref[rows_at(lookup_ref[block, s] * IMG_TOK, IMG_TOK), column : column + HD]
            for s in range(SPAN)
        ],
        axis=0,
    )


def load_table(table_ref, parts):
    size = parts[0].shape[0]
    for at, part in enumerate(parts):
        table_ref[at * size : (at + 1) * size, :] = part[...]


def attend_kernel(blocks, heads, lookup_ref, *refs):
    n = REACH + 1
    parts = refs[:n]
    q_ref, g_ref, scale_ref, seen_ref = refs[n : n + 4]
    ds_ref, coef_ref, own_ref = refs[n + 4 : n + 7]
    back_refs = refs[n + 7 : n + 7 + REACH]
    table_ref, acc_ref, att_ref = refs[n + 7 + REACH :]
    factor = HD ** (-0.5)
    load_table(table_ref, parts)
    acc_ref[...] = jnp.zeros_like(acc_ref)

    def step(block, _):
        keys = cited(lookup_ref, table_ref, block, 0)
        values = cited(lookup_ref, table_ref, block, HD)
        tokens = rows_at(block * BLK, BLK)
        seen = seen_ref[block]
        shown = [(seen > s).astype(f32) for s in range(SPAN)]
        q_rows, g_rows = [], []
        for h in range(heads):
            at = slice(h * HD, (h + 1) * HD)
            q = q_ref[tokens, at]
            g = g_ref[tokens, at]
            q_rows.append(q)
            g_rows.append(g)
            scale = scale_ref[block, h : h + 1, :]
            scale_in = scale * factor
            raw = dot(keys, q, NT)
            grads = dot(values, g, NT)
            powers = jnp.exp2(raw * (scale_in * LOG2E))
            total = sum(
                shown[s] * jnp.sum(powers[s * IMG_TOK : (s + 1) * IMG_TOK], axis=0, keepdims=True)
                for s in range(SPAN)
            )
            inverse = 1.0 / total
            attention = jnp.concatenate(
                [powers[s * IMG_TOK : (s + 1) * IMG_TOK] * (shown[s] * inverse) for s in range(SPAN)],
                axis=0,
            )
            delta = jnp.sum(attention * grads, axis=0, keepdims=True)
            score_grad = attention * (grads - delta) * scale_in
            coef = jnp.sum(score_grad * raw, axis=0, keepdims=True) * (scale * scale * (1.0 / HD))
            coef_ref[block, h : h + 1, :] = coef
            att_ref[:, at] = attention.astype(bf16)
            ds_ref[block, :, at] = score_grad.astype(bf16)
        key_part = dot(ds_ref[block], jnp.concatenate(q_rows, axis=0), NN)
        value_part = dot(att_ref[...], jnp.concatenate(g_rows, axis=0), NN)
        for s in range(SPAN):
            there = rows_at(lookup_ref[block, s] * IMG_TOK, IMG_TOK)
            here = slice(s * IMG_TOK, (s + 1) * IMG_TOK)
            acc_ref[there, :HD] += key_part[here]
            acc_ref[there, HD:] += value_part[here]
        return 0

    lax.fori_loop(0, blocks, step, 0)
    size = own_ref.shape[0]
    own_ref[...] = acc_ref[:size, :]
    for at, ref in enumerate(back_refs):
        ref[...] = acc_ref[(at + 1) * size : (at + 2) * size, :].astype(bf16)


def attend(lookup, parts, queries, out_grad, scales, seen):
    blocks = lookup.shape[0]
    heads = queries.shape[1] // HD
    rows, width = parts[0].shape
    tall = heads * BLK
    args = [lookup, *parts, queries, out_grad, scales, seen]
    return call(
        functools.partial(attend_kernel, blocks, heads),
        [
            jax.ShapeDtypeStruct((blocks, SPAN * IMG_TOK, tall), bf16),
            jax.ShapeDtypeStruct((blocks, heads, BLK), f32),
            jax.ShapeDtypeStruct((rows, width), f32),
        ]
        + [jax.ShapeDtypeStruct((rows, width), bf16)] * REACH,
        args,
        "attend",
        8 * queries.size * HD,
        specs=[SMEM] + [VMEM] * (len(args) - 1),
        scratch_shapes=[
            pltpu.VMEM(((REACH + 1) * rows, width), bf16),
            pltpu.VMEM(((REACH + 1) * rows, width), f32),
            pltpu.VMEM((SPAN * IMG_TOK, tall), bf16),
        ],
    )


def query_kernel(blocks, heads, lookup_ref, *refs):
    n = REACH + 1
    parts = refs[:n]
    q_ref, ds_ref, coef_ref, out_ref, table_ref = refs[n:]
    load_table(table_ref, parts)

    def step(block, _):
        keys = cited(lookup_ref, table_ref, block, 0)
        coef = coef_ref[block].T
        tokens = rows_at(block * BLK, BLK)
        for h in range(heads):
            at = slice(h * HD, (h + 1) * HD)
            part = dot(ds_ref[block, :, at], keys, TN)
            out_ref[tokens, at] = (part - coef[:, h : h + 1] * q_ref[tokens, at].astype(f32)).astype(bf16)
        return 0

    lax.fori_loop(0, blocks, step, 0)


def query_gradient(lookup, parts, queries, score_grads, coefs):
    blocks = lookup.shape[0]
    heads = queries.shape[1] // HD
    rows, width = parts[0].shape
    args = [lookup, *parts, queries, score_grads, coefs]
    return call(
        functools.partial(query_kernel, blocks, heads),
        jax.ShapeDtypeStruct(queries.shape, bf16),
        args,
        "query_gradient",
        2 * queries.size * HD,
        specs=[SMEM] + [VMEM] * (len(args) - 1),
        scratch_shapes=[pltpu.VMEM(((REACH + 1) * rows, width), bf16)],
    )


def round_kernel(*refs):
    own_ref, normed_ref, kscale_ref = refs[:3]
    backs, out_ref = refs[3:-1], refs[-1]
    total = own_ref[...]
    for ref in backs:
        total = total + ref[...].astype(f32)
    normed = normed_ref[...]
    upstream = total[:, :HD]
    mean = jnp.mean(upstream * normed, axis=-1, keepdims=True)
    out_ref[:, :HD] = (kscale_ref[...] * (upstream - normed * mean)).astype(bf16)
    out_ref[:, HD:] = total[:, HD:].astype(bf16)


def round_gradients(own, backs, normed, kscale):
    return call(
        round_kernel,
        jax.ShapeDtypeStruct(own.shape, bf16),
        [own, normed, kscale, *backs],
        "round_gradients",
        own.size * 8,
    )


def image_kernel(count, first, rounds_ref, wk_ref, wv_ref, keep_ref, send_ref):
    own = lax.axis_index("tp")
    size = rounds_ref.shape[0] // count
    half = rounds_ref.shape[0] // 2
    masks = sorted(range(count), key=lambda m: int(bin(m + count)[3:][::-1], 2))
    rows = jnp.concatenate([rounds_ref[rows_at((own ^ m) * size, size), :] for m in masks], axis=0)
    columns = keep_ref.shape[1]
    chunk = min(1024, columns)

    def step(i, _):
        at = rows_at(i * chunk, chunk)
        here = rows_at(first + i * chunk, chunk)
        w = jnp.concatenate([wk_ref[here, :], wv_ref[here, :]], axis=1)
        total = dot(rows, w, NT)
        keep_ref[:, at] = total[:half].astype(bf16)
        send_ref[:, at] = total[half:].astype(bf16)
        return 0

    lax.fori_loop(0, columns // chunk, step, 0)


def image_part(rounds, key_weight, value_weight, count, part, parts):
    rows, width = rounds.shape
    columns = key_weight.shape[0] // parts
    return call(
        functools.partial(image_kernel, count, part * columns),
        [jax.ShapeDtypeStruct((rows // 2, columns), bf16)] * 2,
        [rounds, key_weight, value_weight],
        "image_part",
        4 * rows * columns * HD,
    )


def image_gradient(rounds, key_weight, value_weight, parts):
    count = lax.axis_size("tp")
    outs = []
    for part in range(parts):
        keep, send = image_part(rounds, key_weight, value_weight, count, part, parts)
        bit = 1
        while True:
            keep = keep.astype(f32) + exchanged(send, "tp", bit).astype(f32)
            bit *= 2
            if bit == count:
                break
            half = keep.shape[0] // 2
            keep, send = keep[:half], keep[half:].astype(bf16)
        outs.append(keep.astype(bf16))
    return jnp.concatenate(outs, axis=1)


def weight_kernel(count, *refs):
    states = refs[:count]
    rounds = refs[count:-3]
    key_ref, value_ref, rows_ref = refs[-3:]
    own = lax.axis_index("tp")
    tokens, columns = states[0].shape
    size = tokens // len(rounds)
    chunk = min(256, columns)
    for mask in range(count):
        there = rows_at((own ^ mask) * size, size)
        for at, r in enumerate(rounds):
            rows_ref[mask * tokens + at * size : mask * tokens + (at + 1) * size, :] = r[there, :]

    def step(i, _):
        at = rows_at(i * chunk, chunk)
        x = jnp.concatenate([s[:, at] for s in states], axis=0)
        total = dot(x, rows_ref[...], TN)
        key_ref[at, :] = total[:, :HD]
        value_ref[at, :] = total[:, HD:]
        return 0

    lax.fori_loop(0, columns // chunk, step, 0)


def weight_gradients(states, rounds):
    count = len(states)
    tokens, columns = states[0].shape
    width = rounds[0].shape[1]
    return call(
        functools.partial(weight_kernel, count),
        [jax.ShapeDtypeStruct((columns, HD), f32)] * 2,
        [*states, *rounds],
        "weight_gradients",
        2 * count * tokens * columns * width,
        scratch_shapes=[pltpu.VMEM((count * tokens, width), bf16)],
    )


def on_device(
    queries, out_grad, image_states, key_weight, value_weight, image_spans, visible_images
):
    self_index = lax.axis_index("ctx")
    ctx = lax.axis_size("ctx")
    heads = queries.shape[1] // HD
    blocks = image_spans.shape[0]
    owners = image_spans // IMG_PER_DEV
    lookup = (self_index - owners) * IMG_PER_DEV + image_spans % IMG_PER_DEV
    seen = visible_images.reshape(blocks, 1, BLK)

    pieces = gathered(image_states, "tp")
    scales = query_scales(queries, blocks, heads)

    columns = image_states.shape[1] // ctx
    rows_here = image_states.shape[0]
    if ctx <= 16:
        shares = []
        for mask in range(ctx):
            start = (self_index ^ mask) * columns
            share = lax.dynamic_slice_in_dim(image_states, start, columns, axis=1)
            shares.append(exchanged(share, "ctx", mask) if mask else share)
        share = jnp.concatenate(shares, axis=0)
    else:
        share = lax.all_to_all(image_states, "ctx", split_axis=1, concat_axis=0, tiled=True)
    states = gathered(share, "tp")

    key_values, normed, kscale = project(pieces, key_weight, value_weight)
    parts = [key_values] + [shifted(key_values, "ctx", d) for d in range(1, REACH + 1)]
    score_grads, coefs, own, *windows = attend(lookup, parts, queries, out_grad, scales, seen)
    backs = [shifted(w, "ctx", -d) for d, w in enumerate(windows, 1)]
    query_grad = query_gradient(lookup, parts, queries, score_grads, coefs)
    rounds = round_gradients(own, backs, normed, kscale)
    image_grad = image_gradient(rounds, key_weight, value_weight, 4)
    if ctx <= 16:
        all_rounds = [rounds] + [exchanged(rounds, "ctx", m) for m in range(1, ctx)]
    else:
        all_rounds = list(lax.all_gather(rounds, "ctx"))
    key_weight_grad, value_weight_grad = weight_gradients(states, all_rounds)
    return (query_grad, image_grad, key_weight_grad, value_weight_grad)


def solution(mesh):
    return jax.shard_map(
        on_device,
        mesh=mesh,
        in_specs=(
            P("ctx", "tp"),
            P("ctx", "tp"),
            P(("ctx", "tp"), None),
            P(None, "tp"),
            P(None, "tp"),
            P("ctx", None),
            P("ctx"),
        ),
        out_specs=(P("ctx", "tp"), P(("ctx", "tp"), None), P("ctx", "tp"), P("ctx", "tp")),
        check_vma=False,
    )
```
